32 devices in a mesh: lon: 8 (over z, core), head: 4 (over y, x).
Axes of the slice: x: 2, y: 2, z: 4, core: 2. Of those that a mesh axis runs over, the one named last changes fastest.
Arguments:
- image_tokens: bfloat16 [64, 128, 3072], P(None, 'lon'), may hold values from -6 to 6
- conditioning: bfloat16 [3072], replicated, may hold values from -6 to 6
- mod_weight: bfloat16 [3072, 3, 3072], P(('lon', 'head')), may hold values from -0.21875 to 0.21875
- mod_bias: bfloat16 [3, 3072], replicated, may hold values from -3 to 3
- qkv_weight: bfloat16 [3072, 3, 3072], P('lon', None, 'head'), may hold values from -0.109375 to 0.109375
- qkv_bias: bfloat16 [3, 3072], P(None, 'head'), may hold values from -3 to 3
- q_gain: float32 [128], replicated, may hold values from 0.5 to 12
- k_gain: float32 [128], replicated, may hold values from 0.5 to 12
- text_kv: bfloat16 [2, 512, 3072], P(None, 'lon', 'head'), may hold values from -6 to 6
- proj_weight: bfloat16 [3072, 3072], P('lon', 'head'), may hold values from -0.109375 to 0.109375
- proj_bias: bfloat16 [3072], replicated, may hold values from -3 to 3
Outputs:
- block_output: bfloat16 [64, 128, 3072], P(None, 'lon', 'head')
The draws below stay inside these ranges and needn't reach their ends.
All inputs are finite; a program needn't handle non-finite values.
Results may differ from the reference program's by a relative error of at most 0.0109.
The reference program's roundings to bfloat16 on the way count: a program that leaves them out, or rounds other values in their place, can miss the bound.
Values may be sent and summed in bfloat16 or wider, within the bound.
A program may use at most 128 MiB of HBM per device.

```python
import math
import jax
import jax.numpy as jnp
from jax import lax

D = 3072
HEADS = 24
HD = 128
TXT = 512
LAT = 64
COLS = 16
RADIUS = 15
QROWS = 16
LON = 128


def draw_gain_vector(key):
    return jnp.exp(jax.random.uniform(key, (HD,), jnp.float32, math.log(0.5), math.log(2.0)))


def draw_q_gain(key, part):
    return draw_gain_vector(jax.random.fold_in(key, 101))


def draw_k_gain(key, part):
    return draw_gain_vector(jax.random.fold_in(key, 202))


def raised(values, rng, source, target, parts, factor):
    def block_of(position):
        return (jnp.arange(values.shape[position]) // (values.shape[position] // parts)).reshape((-1,) + (1,) * (values.ndim - 1 - position))

    near = jax.random.permutation(rng, parts)[block_of(target)]
    other_side = (block_of(target) + parts // 2) % parts
    return jnp.where((block_of(source) == near) | (block_of(source) == other_side), factor * values, values)


def block_levels(stream_key, extent, split, low, top_value):
    factor_of, own = 1.0, jax.random.fold_in(stream_key, 6)
    for dim, shards_of in split:
        draws = jnp.exp(jax.random.uniform(jax.random.fold_in(own, dim), (shards_of,), jnp.float32, low / len(split), top_value / len(split)))
        factor_of = factor_of * jnp.repeat(draws, extent[dim] // shards_of).reshape([-1 if axis == dim else 1 for axis in range(len(extent))])
    return factor_of


def bell_draw(rng, extent, width, reach, shards=(), kind=jnp.bfloat16):
    values = width * jax.random.normal(rng, extent, jnp.float32)
    if shards:
        values = values * block_levels(rng, extent, shards, -0.22, 0.18)
    return jnp.clip(values, -reach, reach).astype(kind)


def gaussian_with(key, shape, width, bound, pieces, heavy, kind=jnp.bfloat16):
    values = width * jax.random.normal(key, shape, jnp.float32)
    if pieces:
        values = values * block_levels(key, shape, pieces, -0.22, 0.18)
    return jnp.clip(raised(values, jax.random.fold_in(key, 3), *heavy), -bound, bound).astype(kind)


def setup_inputs(seed: int = 0) -> dict:
    key_of = jax.random.split(jax.random.key(seed), 12)
    return {
        "image_tokens": bell_draw(key_of[0], (LAT, LON, D), 1.0, 6.0, ((1, 8),)),
        "conditioning": bell_draw(key_of[1], (D,), 1.0, 6.0),
        "mod_weight": gaussian_with(key_of[2], (D, 3, D), D ** -0.5, 0.21875, ((0, 32),), (0, 2, 32, 2.75)),
        "mod_bias": bell_draw(key_of[3], (3, D), 0.5, 3.0),
        "qkv_weight": bell_draw(key_of[4], (D, 3, HEADS * HD), D ** -0.5, 0.109375, ((0, 8), (2, 4))),
        "qkv_bias": bell_draw(key_of[5], (3, HEADS * HD), 0.5, 3.0, ((1, 4),)),
        "q_gain": draw_q_gain(jax.random.fold_in(key_of[11], 71), 0),
        "k_gain": draw_k_gain(jax.random.fold_in(key_of[11], 71), 0),
        "text_kv": bell_draw(key_of[8], (2, TXT, HEADS * HD), 1.0, 6.0, ((1, 8), (2, 4))),
        "proj_weight": bell_draw(key_of[9], (HEADS * HD, D), (HEADS * HD) ** -0.5, 0.109375, ((0, 8), (1, 4))),
        "proj_bias": bell_draw(key_of[10], (D,), 0.5, 3.0),
    }


def rms_scale(entries, gain):
    mean_square = lax.optimization_barrier(jnp.mean(entries * entries, axis=-1, keepdims=True))
    return entries * lax.rsqrt(mean_square + 1e-06) * gain

def window_mask(row_first, q_rows, q_cols, k_rows, k_cols, lat_total):
    query_index = jnp.arange(q_rows * q_cols, dtype=jnp.int32)
    key_index = jnp.arange(k_rows * k_cols, dtype=jnp.int32)
    query_row = (query_index // q_cols)[:, None]
    query_col = (query_index % q_cols)[:, None]
    key_row = (key_index // k_cols)[None, :]
    key_col = (key_index % k_cols)[None, :]
    global_row = row_first + key_row - RADIUS
    near_rows = jnp.abs(key_row - RADIUS - query_row) <= RADIUS
    near_cols = jnp.abs(key_col - RADIUS - query_col) <= RADIUS
    inside = (global_row >= 0) & (global_row < lat_total)
    return near_rows & near_cols & inside

def attend(queries, key_block, value_block, text_keys, text_values, row_first):
    q_rows, q_cols, heads_here, head_dim = queries.shape
    k_rows, k_cols = (key_block.shape[0], key_block.shape[1])
    flat_query = queries.reshape(q_rows * q_cols, heads_here, head_dim).astype(jnp.float32)
    flat_keys = key_block.reshape(k_rows * k_cols, heads_here, head_dim).astype(jnp.float32)
    flat_values = value_block.reshape(k_rows * k_cols, heads_here, head_dim).astype(jnp.float32)
    factor = 1.0 / math.sqrt(head_dim)
    image_scores = jnp.einsum('qhd,khd->hqk', flat_query, flat_keys) * factor
    text_scores = jnp.einsum('qhd,khd->hqk', flat_query, text_keys.astype(jnp.float32)) * factor
    allowed = window_mask(row_first, q_rows, q_cols, k_rows, k_cols, LAT)
    image_scores = jnp.where(allowed[None], image_scores, -jnp.inf)
    highest = jnp.maximum(lax.optimization_barrier(jnp.max(image_scores, axis=2, keepdims=True)), lax.optimization_barrier(jnp.max(text_scores, axis=2, keepdims=True)))
    image_exp = jnp.exp(image_scores - highest)
    text_exp = jnp.exp(text_scores - highest)
    normaliser = lax.optimization_barrier(jnp.sum(image_exp, axis=2, keepdims=True)) + lax.optimization_barrier(jnp.sum(text_exp, axis=2, keepdims=True))
    image_probs = (image_exp / normaliser).astype(jnp.bfloat16)
    text_probs = (text_exp / normaliser).astype(jnp.bfloat16)
    combined = jnp.einsum('hqk,khd->qhd', image_probs.astype(jnp.float32), flat_values)
    combined = combined + jnp.einsum('hqk,khd->qhd', text_probs.astype(jnp.float32), text_values.astype(jnp.float32))
    return combined.astype(jnp.bfloat16).reshape(q_rows, q_cols, heads_here * head_dim)

def reference(image_tokens, conditioning, mod_weight, mod_bias, qkv_weight, qkv_bias, q_gain, k_gain, text_kv, proj_weight, proj_bias):
    model_width = D
    inner_width = HEADS * HD
    silu_cond = jax.nn.silu(conditioning.astype(jnp.float32))
    modulation = jnp.dot(silu_cond, mod_weight.reshape(model_width, 3 * model_width).astype(jnp.float32), precision=lax.Precision.HIGHEST)
    modulation = modulation.reshape(3, model_width) + mod_bias.astype(jnp.float32)
    shift_row, scale_row, gate_row = (modulation[0], modulation[1], modulation[2])
    token_values = image_tokens.astype(jnp.float32).reshape(LAT * LON, model_width)
    average = lax.optimization_barrier(jnp.mean(token_values, axis=1, keepdims=True))
    centred = token_values - average
    variance = lax.optimization_barrier(jnp.mean(centred * centred, axis=1, keepdims=True))
    modulated = ((1.0 + scale_row) * (centred * lax.rsqrt(variance + 1e-06)) + shift_row).astype(jnp.bfloat16)
    projected = jnp.dot(modulated, qkv_weight.reshape(model_width, 3 * inner_width), preferred_element_type=jnp.float32)
    projected = projected.reshape(LAT * LON, 3, inner_width) + qkv_bias.astype(jnp.float32)
    queries = rms_scale(projected[:, 0].reshape(LAT, LON, HEADS, HD), q_gain).astype(jnp.bfloat16)
    keys_normed = rms_scale(projected[:, 1].reshape(LAT, LON, HEADS, HD), k_gain).astype(jnp.bfloat16)
    values_image = projected[:, 2].reshape(LAT, LON, HEADS, HD).astype(jnp.bfloat16)

    def widen(field):
        wrapped = jnp.concatenate([field[:, LON - RADIUS:], field, field[:, :RADIUS]], axis=1)
        return jnp.pad(wrapped, ((RADIUS, RADIUS), (0, 0), (0, 0), (0, 0)))
    padded_keys = widen(keys_normed)
    padded_values = widen(values_image)
    text_keys = text_kv[0].reshape(TXT, HEADS, HD)
    text_values = text_kv[1].reshape(TXT, HEADS, HD)
    col_blocks = LON // COLS
    block_count = LAT // QROWS * col_blocks
    zero_index = jnp.int32(0)

    def one_block(block_index):
        row_first = block_index // col_blocks * QROWS
        col_first = block_index % col_blocks * COLS
        query_block = lax.dynamic_slice(queries, (row_first, col_first, zero_index, zero_index), (QROWS, COLS, HEADS, HD))
        key_block = lax.dynamic_slice(padded_keys, (row_first, col_first, zero_index, zero_index), (QROWS + 2 * RADIUS, COLS + 2 * RADIUS, HEADS, HD))
        value_block = lax.dynamic_slice(padded_values, (row_first, col_first, zero_index, zero_index), (QROWS + 2 * RADIUS, COLS + 2 * RADIUS, HEADS, HD))
        return attend(query_block, key_block, value_block, text_keys, text_values, row_first)
    blocks = lax.map(one_block, jnp.arange(block_count, dtype=jnp.int32))
    blocks = blocks.reshape(LAT // QROWS, col_blocks, QROWS, COLS, inner_width)
    attended = jnp.transpose(blocks, (0, 2, 1, 3, 4)).reshape(LAT * LON, inner_width)
    out_sum = jnp.dot(attended, proj_weight, preferred_element_type=jnp.float32) + proj_bias.astype(jnp.float32)
    block_output = (token_values + gate_row * out_sum).astype(jnp.bfloat16)
    return block_output.reshape(LAT, LON, model_width)
```

```python
import functools
import math

import jax
import jax.numpy as jnp
from jax import lax
from jax.experimental import pallas as pl
from jax.experimental.pallas import tpu as pltpu
from jax.sharding import PartitionSpec as P

RADIUS = 15
QROWS = 16
VMEM_LIMIT = 56 * 1024 * 1024


def proj_kernel(normed, head_dim, x_ref, w_ref, b_ref, g_ref, o_ref):
    rows, width = o_ref.shape
    step = min(256, rows)

    def one(i, carry):
        at = pl.ds(pl.multiple_of(i * step, step), step)
        raw = jnp.dot(x_ref[at, :], w_ref[...], preferred_element_type=jnp.float32) + b_ref[...]
        if normed:
            for h in range(width // head_dim):
                cols = slice(h * head_dim, (h + 1) * head_dim)
                entries = raw[:, cols]
                mean_square = jnp.mean(entries * entries, axis=-1, keepdims=True)
                scaled = entries * lax.rsqrt(mean_square + 1e-06) * g_ref[...]
                o_ref[at, cols] = scaled.astype(o_ref.dtype)
        else:
            o_ref[at, :] = raw.astype(o_ref.dtype)
        return carry

    lax.fori_loop(0, rows // step, one, 0)


def project(x, w, first, bias, gain, normed):
    rows, depth = x.shape
    inner, head_dim = bias.shape[0], gain.shape[0]
    width = 2 * head_dim if inner % (2 * head_dim) == 0 else head_dim
    off = first // width
    return pl.pallas_call(
        functools.partial(proj_kernel, normed, head_dim),
        out_shape=jax.ShapeDtypeStruct((rows, inner), jnp.bfloat16),
        grid=(inner // width,),
        in_specs=[
            pl.BlockSpec((rows, depth), lambda j: (0, 0), pipeline_mode=pl.Buffered(1)),
            pl.BlockSpec((depth, width), lambda j: (0, off + j)),
            pl.BlockSpec((1, width), lambda j: (0, j)),
            pl.BlockSpec((1, head_dim), lambda j: (0, 0)),
        ],
        out_specs=pl.BlockSpec((rows, width), lambda j: (0, j)),
        compiler_params=pltpu.CompilerParams(vmem_limit_bytes=VMEM_LIMIT),
        cost_estimate=pl.CostEstimate(
            flops=2 * rows * depth * inner,
            bytes_accessed=2 * (rows * depth + depth * inner + rows * inner),
            transcendentals=0,
        ),
    )(x, w, bias.reshape(1, inner), gain.reshape(1, head_dim))


def attn_kernel(
    q_blocks, row_blocks, cols, q_ref, kc, vc, kl, vl, kr, vr, tk, tv, o_ref, bias_ref
):
    block = QROWS * cols
    head_dim = q_ref.shape[1]
    factor = math.log2(math.e) / math.sqrt(head_dim)

    @pl.when(pl.program_id(0) == 0)
    def _():
        query = lax.broadcasted_iota(jnp.int32, (block, 3 * block), 0)
        key = lax.broadcasted_iota(jnp.int32, (block, 3 * block), 1)
        row_gap = key // cols - QROWS - query // cols
        for side in range(3):
            col_gap = key % cols + (side - 1) * cols - query % cols
            near = (jnp.abs(row_gap) <= RADIUS) & (jnp.abs(col_gap) <= RADIUS)
            bias_ref[side] = jnp.where(near, 0.0, -1e30).astype(jnp.float32)

    contract = (((1,), (1,)), ((), ()))
    for n, qb in enumerate(q_blocks):
        low, high = max(qb - 1, 0), min(qb + 2, row_blocks)
        first = (low - qb + 1) * block
        width = (high - low) * block
        q = q_ref[n * block : (n + 1) * block, :]
        scores = []
        values = []
        for side, (k_ref, v_ref) in enumerate(((kl, vl), (kc, vc), (kr, vr))):
            k = k_ref[low * block : high * block, :]
            s = lax.dot_general(q, k, contract, preferred_element_type=jnp.float32)
            scores.append(s + bias_ref[side, :, first : first + width])
            values.append(v_ref[low * block : high * block, :])
        scores.append(lax.dot_general(q, tk[...], contract, preferred_element_type=jnp.float32))
        values.append(tv[...])
        highest = functools.reduce(
            jnp.maximum, [jnp.max(s, axis=1, keepdims=True) for s in scores]
        )
        total = 0.0
        out = 0.0
        for s, v in zip(scores, values):
            p = jnp.exp2((s - highest) * factor)
            total = total + jnp.sum(p, axis=1, keepdims=True)
            out = out + jnp.dot(p.astype(jnp.bfloat16), v, preferred_element_type=jnp.float32)
        o_ref[n * block : (n + 1) * block, :] = (out / total).astype(o_ref.dtype)


def attend(q, own, left, right, text, head_dim, cols, part, parts):
    rows, inner = q.shape
    block = QROWS * cols
    row_blocks = rows // block
    per = row_blocks // parts
    q_blocks = tuple(range(part * per, (part + 1) * per))
    text_count = text[0].shape[0]
    whole = pl.BlockSpec((rows, head_dim), lambda h: (0, h))
    texts = pl.BlockSpec((text_count, head_dim), lambda h: (0, h))
    pairs = per * block * (9 * block + text_count)
    return pl.pallas_call(
        functools.partial(attn_kernel, q_blocks, row_blocks, cols),
        out_shape=jax.ShapeDtypeStruct((per * block, inner), jnp.bfloat16),
        grid=(inner // head_dim,),
        in_specs=[pl.BlockSpec((per * block, head_dim), lambda h: (part, h))]
        + [whole] * 6
        + [texts] * 2,
        out_specs=pl.BlockSpec((per * block, head_dim), lambda h: (0, h)),
        scratch_shapes=[pltpu.VMEM((3, block, 3 * block), jnp.float32)],
        compiler_params=pltpu.CompilerParams(vmem_limit_bytes=VMEM_LIMIT),
        cost_estimate=pl.CostEstimate(
            flops=4 * pairs * inner,
            bytes_accessed=2 * (6 * rows * inner + 2 * text_count * inner + 2 * per * block * inner),
            transcendentals=pairs * (inner // head_dim),
        ),
    )(q, *own, *left, *right, *text)


def out_kernel(parts, a_ref, w_ref, image_ref, gate_ref, bias_ref, o_ref):
    inner = a_ref.shape[2]
    total = bias_ref[...]
    for g in range(parts):
        total = total + jnp.dot(
            a_ref[g], w_ref[g * inner : (g + 1) * inner, :], preferred_element_type=jnp.float32
        )
    o_ref[...] = (image_ref[...].astype(jnp.float32) + gate_ref[...] * total).astype(o_ref.dtype)


def output(gathered, w, image, first, gate, bias):
    groups, rows, inner = gathered.shape
    cols = w.shape[1]
    step = 256
    off = first // step
    return pl.pallas_call(
        functools.partial(out_kernel, groups),
        out_shape=jax.ShapeDtypeStruct((rows, cols), jnp.bfloat16),
        grid=(rows // step,),
        in_specs=[
            pl.BlockSpec((groups, step, inner), lambda i: (0, i, 0)),
            pl.BlockSpec(w.shape, lambda i: (0, 0), pipeline_mode=pl.Buffered(1)),
            pl.BlockSpec((step, cols), lambda i: (off + i, 0)),
            pl.BlockSpec((1, cols), lambda i: (0, 0)),
            pl.BlockSpec((1, cols), lambda i: (0, 0)),
        ],
        out_specs=pl.BlockSpec((step, cols), lambda i: (i, 0)),
        compiler_params=pltpu.CompilerParams(vmem_limit_bytes=VMEM_LIMIT),
        cost_estimate=pl.CostEstimate(
            flops=2 * rows * groups * inner * cols,
            bytes_accessed=2 * (groups * inner * (rows + cols) + 2 * rows * cols),
            transcendentals=0,
        ),
    )(gathered, w, image, gate.reshape(1, cols), bias.reshape(1, cols))


def body(
    image_tokens,
    conditioning,
    mod_weight,
    mod_bias,
    qkv_weight,
    qkv_bias,
    q_gain,
    k_gain,
    text_kv,
    proj_weight,
    proj_bias,
):
    lat_rows, col_count, model_width = image_tokens.shape
    token_count = lat_rows * col_count
    head_groups = lax.axis_size("head")
    inner_here = qkv_weight.shape[2]
    flat_weight = qkv_weight.reshape(qkv_weight.shape[0], 3 * inner_here)
    kv_rows = lax.all_gather(flat_weight[:, inner_here:], "lon", axis=0, tiled=True)
    q_rows = lax.all_gather(flat_weight[:, :inner_here], "lon", axis=0, tiled=True)
    text_panel = lax.all_gather(text_kv, "lon", axis=1, tiled=True)
    proj_columns = lax.all_gather(proj_weight, "lon", axis=0, tiled=True)
    slice_rows = mod_weight.shape[0]
    row_offset = (lax.axis_index("lon") * head_groups + lax.axis_index("head")) * slice_rows
    silu_part = jax.nn.silu(
        lax.dynamic_slice_in_dim(conditioning, row_offset, slice_rows, 0).astype(jnp.float32)
    )
    partial_mod = jnp.dot(
        silu_part,
        mod_weight.reshape(slice_rows, 3 * model_width).astype(jnp.float32),
        precision=lax.Precision.HIGHEST,
    )
    modulation = lax.psum(partial_mod, ("lon", "head")).reshape(3, model_width) + mod_bias.astype(
        jnp.float32
    )
    token_values = image_tokens.reshape(token_count, model_width).astype(jnp.float32)
    average = jnp.mean(token_values, axis=1, keepdims=True)
    centred = token_values - average
    variance = jnp.mean(centred * centred, axis=1, keepdims=True)
    modulated = (
        (1.0 + modulation[1]) * (centred * lax.rsqrt(variance + 1e-06)) + modulation[0]
    ).astype(jnp.bfloat16)
    local_inner = qkv_weight.shape[2]
    head_dim = q_gain.shape[0]
    bias = qkv_bias.astype(jnp.float32)
    own_k = project(modulated, kv_rows, 0, bias[1], k_gain, True)
    own_v = project(modulated, kv_rows, local_inner, bias[2], k_gain, False)
    count = lax.axis_size("lon")
    up = [(i, (i + 1) % count) for i in range(count)]
    down = [((i + 1) % count, i) for i in range(count)]
    left = (lax.ppermute(own_k, "lon", up), lax.ppermute(own_v, "lon", up))
    right = (lax.ppermute(own_k, "lon", down), lax.ppermute(own_v, "lon", down))
    queries = project(modulated, q_rows, 0, bias[0], q_gain, True)
    out_cols = model_width // head_groups
    col_offset = lax.axis_index("head") * out_cols
    own_image = lax.dynamic_slice_in_dim(
        image_tokens.reshape(token_count, model_width), col_offset, out_cols, 1
    )
    own_gate = lax.dynamic_slice_in_dim(modulation[2], col_offset, out_cols, 0)
    own_bias = lax.dynamic_slice_in_dim(proj_bias, col_offset, out_cols, 0).astype(jnp.float32)
    text = (text_panel[0], text_panel[1])
    parts = 2
    rows = token_count // parts
    outs = []
    for part in range(parts):
        attended = attend(
            queries, (own_k, own_v), left, right, text, head_dim, col_count, part, parts
        )
        gathered = lax.all_gather(attended, "head", axis=0)
        outs.append(output(gathered, proj_columns, own_image, part * rows, own_gate, own_bias))
    block_output = jnp.concatenate(outs, axis=0)
    return block_output.reshape(lat_rows, col_count, out_cols)


def solution(mesh):
    placed = (
        P(None, "lon", None),
        P(),
        P(("lon", "head"), None, None),
        P(),
        P("lon", None, "head"),
        P(None, "head"),
        P(),
        P(),
        P(None, "lon", "head"),
        P("lon", "head"),
        P(),
    )
    return jax.shard_map(
        body, mesh=mesh, in_specs=placed, out_specs=P(None, "lon", "head"), check_vma=False
    )
```

```python
import functools
import math

import jax
import jax.numpy as jnp
from jax import lax
from jax.experimental import pallas as pl
from jax.experimental.pallas import tpu as pltpu
from jax.sharding import PartitionSpec as P

RADIUS = 15
QROWS = 16
VMEM_LIMIT = 56 * 1024 * 1024


def proj_kernel(normed, head_dim, x_ref, w_ref, b_ref, g_ref, o_ref):
    rows, width = o_ref.shape
    step = min(256, rows)

    def one(i, carry):
        at = pl.ds(pl.multiple_of(i * step, step), step)
        raw = jnp.dot(x_ref[at, :], w_ref[...], preferred_element_type=jnp.float32) + b_ref[...]
        if normed:
            for h in range(width // head_dim):
                cols = slice(h * head_dim, (h + 1) * head_dim)
                entries = raw[:, cols]
                mean_square = jnp.mean(entries * entries, axis=-1, keepdims=True)
                scaled = entries * lax.rsqrt(mean_square + 1e-06) * g_ref[...]
                o_ref[at, cols] = scaled.astype(o_ref.dtype)
        else:
            o_ref[at, :] = raw.astype(o_ref.dtype)
        return carry

    lax.fori_loop(0, rows // step, one, 0)


def project(x, w, first, bias, gain, normed):
    rows, depth = x.shape
    inner, head_dim = bias.shape[0], gain.shape[0]
    width = 2 * head_dim if inner % (2 * head_dim) == 0 else head_dim
    off = first // width
    return pl.pallas_call(
        functools.partial(proj_kernel, normed, head_dim),
        out_shape=jax.ShapeDtypeStruct((rows, inner), jnp.bfloat16),
        grid=(inner // width,),
        in_specs=[
            pl.BlockSpec((rows, depth), lambda j: (0, 0), pipeline_mode=pl.Buffered(1)),
            pl.BlockSpec((depth, width), lambda j: (0, off + j)),
            pl.BlockSpec((1, width), lambda j: (0, j)),
            pl.BlockSpec((1, head_dim), lambda j: (0, 0)),
        ],
        out_specs=pl.BlockSpec((rows, width), lambda j: (0, j)),
        compiler_params=pltpu.CompilerParams(vmem_limit_bytes=VMEM_LIMIT),
        cost_estimate=pl.CostEstimate(
            flops=2 * rows * depth * inner,
            bytes_accessed=2 * (rows * depth + depth * inner + rows * inner),
            transcendentals=0,
        ),
    )(x, w, bias.reshape(1, inner), gain.reshape(1, head_dim))


def attn_kernel(
    q_blocks, row_blocks, cols, q_ref, kc, vc, kl, vl, kr, vr, tk, tv, o_ref, bias_ref
):
    block = QROWS * cols
    head_dim = q_ref.shape[1]
    factor = math.log2(math.e) / math.sqrt(head_dim)

    @pl.when(pl.program_id(0) == 0)
    def _():
        query = lax.broadcasted_iota(jnp.int32, (block, 3 * block), 0)
        key = lax.broadcasted_iota(jnp.int32, (block, 3 * block), 1)
        row_gap = key // cols - QROWS - query // cols
        for side in range(3):
            col_gap = key % cols + (side - 1) * cols - query % cols
            near = (jnp.abs(row_gap) <= RADIUS) & (jnp.abs(col_gap) <= RADIUS)
            bias_ref[side] = jnp.where(near, 0.0, -1e30).astype(jnp.float32)

    contract = (((1,), (1,)), ((), ()))
    for n, qb in enumerate(q_blocks):
        low, high = max(qb - 1, 0), min(qb + 2, row_blocks)
        first = (low - qb + 1) * block
        width = (high - low) * block
        q = q_ref[n * block : (n + 1) * block, :]
        scores = []
        values = []
        for side, (k_ref, v_ref) in enumerate(((kl, vl), (kc, vc), (kr, vr))):
            k = k_ref[low * block : high * block, :]
            s = lax.dot_general(q, k, contract, preferred_element_type=jnp.float32)
            scores.append(s + bias_ref[side, :, first : first + width])
            values.append(v_ref[low * block : high * block, :])
        scores.append(lax.dot_general(q, tk[...], contract, preferred_element_type=jnp.float32))
        values.append(tv[...])
        highest = functools.reduce(
            jnp.maximum, [jnp.max(s, axis=1, keepdims=True) for s in scores]
        )
        total = 0.0
        out = 0.0
        for s, v in zip(scores, values):
            p = jnp.exp2((s - highest) * factor)
            total = total + jnp.sum(p, axis=1, keepdims=True)
            out = out + jnp.dot(p.astype(jnp.bfloat16), v, preferred_element_type=jnp.float32)
        o_ref[n * block : (n + 1) * block, :] = (out / total).astype(o_ref.dtype)


def attend(q, own, left, right, text, head_dim, cols, part, parts):
    rows, inner = q.shape
    block = QROWS * cols
    row_blocks = rows // block
    per = row_blocks // parts
    q_blocks = tuple(range(part * per, (part + 1) * per))
    text_count = text[0].shape[0]
    whole = pl.BlockSpec((rows, head_dim), lambda h: (0, h))
    texts = pl.BlockSpec((text_count, head_dim), lambda h: (0, h))
    pairs = per * block * (9 * block + text_count)
    return pl.pallas_call(
        functools.partial(attn_kernel, q_blocks, row_blocks, cols),
        out_shape=jax.ShapeDtypeStruct((per * block, inner), jnp.bfloat16),
        grid=(inner // head_dim,),
        in_specs=[pl.BlockSpec((per * block, head_dim), lambda h: (part, h))]
        + [whole] * 6
        + [texts] * 2,
        out_specs=pl.BlockSpec((per * block, head_dim), lambda h: (0, h)),
        scratch_shapes=[pltpu.VMEM((3, block, 3 * block), jnp.float32)],
        compiler_params=pltpu.CompilerParams(vmem_limit_bytes=VMEM_LIMIT),
        cost_estimate=pl.CostEstimate(
            flops=4 * pairs * inner,
            bytes_accessed=2 * (6 * rows * inner + 2 * text_count * inner + 2 * per * block * inner),
            transcendentals=pairs * (inner // head_dim),
        ),
    )(q, *own, *left, *right, *text)


def out_kernel(groups, me_ref, *refs):
    a_refs = refs[:groups]
    w_ref, image_ref, gate_ref, bias_ref = refs[groups : groups + 4]
    o_ref = refs[-1]
    inner = a_refs[0].shape[1]
    total = bias_ref[...]
    for k in range(groups):
        row = pl.multiple_of(peer(me_ref[0], k, groups) * inner, inner)
        total = total + jnp.dot(
            a_refs[k][...], w_ref[pl.ds(row, inner), :], preferred_element_type=jnp.float32
        )
    o_ref[...] = (image_ref[...].astype(jnp.float32) + gate_ref[...] * total).astype(o_ref.dtype)


def peer(me, k, groups):
    if groups & (groups - 1) == 0:
        return me ^ k
    return (me + k) % groups


def exchange(block):
    groups = lax.axis_size("head")
    return [block] + [
        lax.ppermute(block, "head", [(peer(i, k, groups), i) for i in range(groups)])
        for k in range(1, groups)
    ]


def output(gathered, w, image, first, gate, bias, before):
    groups = len(gathered)
    rows, inner = gathered[0].shape
    cols = w.shape[1]
    step = 256
    off = first // step
    here = pl.BlockSpec((step, cols), lambda i: (off + i, 0))
    row = pl.BlockSpec((1, cols), lambda i: (0, 0))
    operands = [lax.axis_index("head").astype(jnp.int32).reshape(1), *gathered, w, image]
    operands += [gate.reshape(1, cols), bias.reshape(1, cols)]
    specs = [pl.BlockSpec(memory_space=pltpu.SMEM)]
    specs += [pl.BlockSpec((step, inner), lambda i: (i, 0))] * groups
    specs += [pl.BlockSpec(w.shape, lambda i: (0, 0), pipeline_mode=pl.Buffered(1)), here, row, row]
    aliases = {}
    if before is not None:
        aliases = {len(operands): 0}
        operands.append(before)
        specs.append(pl.BlockSpec(memory_space=pl.ANY))
    return pl.pallas_call(
        functools.partial(out_kernel, groups),
        out_shape=jax.ShapeDtypeStruct(image.shape, jnp.bfloat16),
        grid=(rows // step,),
        in_specs=specs,
        out_specs=here,
        input_output_aliases=aliases,
        compiler_params=pltpu.CompilerParams(vmem_limit_bytes=VMEM_LIMIT),
        cost_estimate=pl.CostEstimate(
            flops=2 * rows * groups * inner * cols,
            bytes_accessed=2 * (groups * inner * (rows + cols) + 2 * rows * cols),
            transcendentals=0,
        ),
    )(*operands)


def body(
    image_tokens,
    conditioning,
    mod_weight,
    mod_bias,
    qkv_weight,
    qkv_bias,
    q_gain,
    k_gain,
    text_kv,
    proj_weight,
    proj_bias,
):
    lat_rows, col_count, model_width = image_tokens.shape
    token_count = lat_rows * col_count
    head_groups = lax.axis_size("head")
    inner_here = qkv_weight.shape[2]
    flat_weight = qkv_weight.reshape(qkv_weight.shape[0], 3 * inner_here)
    gather_rows = functools.partial(lax.all_gather, axis_name="lon", axis=0, tiled=True)
    k_rows = gather_rows(flat_weight[:, inner_here : 2 * inner_here])
    v_rows = gather_rows(flat_weight[:, 2 * inner_here :])
    k_rows, q_here = lax.optimization_barrier((k_rows, flat_weight[:, :inner_here]))
    q_rows = gather_rows(q_here)
    v_rows, text_here = lax.optimization_barrier((v_rows, text_kv))
    text_panel = lax.all_gather(text_here, "lon", axis=1, tiled=True)
    q_rows, proj_here = lax.optimization_barrier((q_rows, proj_weight))
    proj_columns = gather_rows(proj_here)
    slice_rows = mod_weight.shape[0]
    row_offset = (lax.axis_index("lon") * head_groups + lax.axis_index("head")) * slice_rows
    silu_part = jax.nn.silu(
        lax.dynamic_slice_in_dim(conditioning, row_offset, slice_rows, 0).astype(jnp.float32)
    )
    partial_mod = jnp.dot(
        silu_part,
        mod_weight.reshape(slice_rows, 3 * model_width).astype(jnp.float32),
        precision=lax.Precision.HIGHEST,
    )
    modulation = lax.psum(partial_mod, ("lon", "head")).reshape(3, model_width) + mod_bias.astype(
        jnp.float32
    )
    token_values = image_tokens.reshape(token_count, model_width).astype(jnp.float32)
    average = jnp.mean(token_values, axis=1, keepdims=True)
    centred = token_values - average
    variance = jnp.mean(centred * centred, axis=1, keepdims=True)
    modulated = (
        (1.0 + modulation[1]) * (centred * lax.rsqrt(variance + 1e-06)) + modulation[0]
    ).astype(jnp.bfloat16)
    local_inner = qkv_weight.shape[2]
    head_dim = q_gain.shape[0]
    bias = qkv_bias.astype(jnp.float32)
    own_k = project(modulated, k_rows, 0, bias[1], k_gain, True)
    own_v = project(modulated, v_rows, 0, bias[2], k_gain, False)
    count = lax.axis_size("lon")
    up = [(i, (i + 1) % count) for i in range(count)]
    down = [((i + 1) % count, i) for i in range(count)]
    left = (lax.ppermute(own_k, "lon", up), lax.ppermute(own_v, "lon", up))
    right = (lax.ppermute(own_k, "lon", down), lax.ppermute(own_v, "lon", down))
    queries = project(modulated, q_rows, 0, bias[0], q_gain, True)
    out_cols = model_width // head_groups
    col_offset = lax.axis_index("head") * out_cols
    own_image = lax.dynamic_slice_in_dim(
        image_tokens.reshape(token_count, model_width), col_offset, out_cols, 1
    )
    own_gate = lax.dynamic_slice_in_dim(modulation[2], col_offset, out_cols, 0)
    own_bias = lax.dynamic_slice_in_dim(proj_bias, col_offset, out_cols, 0).astype(jnp.float32)
    text = (text_panel[0], text_panel[1])
    parts = lat_rows // QROWS
    rows = token_count // parts
    blocks = []
    for part in range(parts):
        attended = attend(
            queries, (own_k, own_v), left, right, text, head_dim, col_count, part, parts
        )
        blocks.append(exchange(attended))
    block_output = None
    for part, gathered in enumerate(blocks):
        block_output = output(
            gathered, proj_columns, own_image, part * rows, own_gate, own_bias, block_output
        )
    return block_output.reshape(lat_rows, col_count, out_cols)


def solution(mesh):
    placed = (
        P(None, "lon", None),
        P(),
        P(("lon", "head"), None, None),
        P(),
        P("lon", None, "head"),
        P(None, "head"),
        P(),
        P(),
        P(None, "lon", "head"),
        P("lon", "head"),
        P(),
    )
    return jax.shard_map(
        body, mesh=mesh, in_specs=placed, out_specs=P(None, "lon", "head"), check_vma=False
    )
```

```python
import functools
import math

import jax
import jax.numpy as jnp
from jax import lax
from jax.experimental import pallas as pl
from jax.experimental.pallas import tpu as pltpu
from jax.sharding import PartitionSpec as P

RADIUS = 15
QROWS = 16
VMEM_LIMIT = 56 * 1024 * 1024


def proj_kernel(normed, head_dim, x_ref, w_ref, b_ref, g_ref, o_ref):
    rows, width = o_ref.shape
    step = min(256, rows)

    def one(i, carry):
        at = pl.ds(pl.multiple_of(i * step, step), step)
        raw = jnp.dot(x_ref[at, :], w_ref[...], preferred_element_type=jnp.float32) + b_ref[...]
        if normed:
            for h in range(width // head_dim):
                cols = slice(h * head_dim, (h + 1) * head_dim)
                entries = raw[:, cols]
                mean_square = jnp.mean(entries * entries, axis=-1, keepdims=True)
                scaled = entries * lax.rsqrt(mean_square + 1e-06) * g_ref[...]
                o_ref[at, cols] = scaled.astype(o_ref.dtype)
        else:
            o_ref[at, :] = raw.astype(o_ref.dtype)
        return carry

    lax.fori_loop(0, rows // step, one, 0)


def project(x, w, first, bias, gain, normed):
    rows, depth = x.shape
    inner, head_dim = bias.shape[0], gain.shape[0]
    width = 2 * head_dim if inner % (2 * head_dim) == 0 else head_dim
    off = first // width
    return pl.pallas_call(
        functools.partial(proj_kernel, normed, head_dim),
        out_shape=jax.ShapeDtypeStruct((rows, inner), jnp.bfloat16),
        grid=(inner // width,),
        in_specs=[
            pl.BlockSpec((rows, depth), lambda j: (0, 0), pipeline_mode=pl.Buffered(1)),
            pl.BlockSpec((depth, width), lambda j: (0, off + j)),
            pl.BlockSpec((1, width), lambda j: (0, j)),
            pl.BlockSpec((1, head_dim), lambda j: (0, 0)),
        ],
        out_specs=pl.BlockSpec((rows, width), lambda j: (0, j)),
        compiler_params=pltpu.CompilerParams(vmem_limit_bytes=VMEM_LIMIT),
        cost_estimate=pl.CostEstimate(
            flops=2 * rows * depth * inner,
            bytes_accessed=2 * (rows * depth + depth * inner + rows * inner),
            transcendentals=0,
        ),
    )(x, w, bias.reshape(1, inner), gain.reshape(1, head_dim))


def attn_kernel(
    q_blocks, row_blocks, cols, q_ref, kc, vc, kl, vl, kr, vr, tk, tv, o_ref, bias_ref
):
    block = QROWS * cols
    head_dim = q_ref.shape[1]
    factor = math.log2(math.e) / math.sqrt(head_dim)

    @pl.when(pl.program_id(0) == 0)
    def _():
        query = lax.broadcasted_iota(jnp.int32, (block, 3 * block), 0)
        key = lax.broadcasted_iota(jnp.int32, (block, 3 * block), 1)
        row_gap = key // cols - QROWS - query // cols
        for side in range(3):
            col_gap = key % cols + (side - 1) * cols - query % cols
            near = (jnp.abs(row_gap) <= RADIUS) & (jnp.abs(col_gap) <= RADIUS)
            bias_ref[side] = jnp.where(near, 0.0, -1e30).astype(jnp.float32)

    contract = (((1,), (1,)), ((), ()))
    for n, qb in enumerate(q_blocks):
        low, high = max(qb - 1, 0), min(qb + 2, row_blocks)
        first = (low - qb + 1) * block
        width = (high - low) * block
        q = q_ref[n * block : (n + 1) * block, :]
        scores = []
        values = []
        for side, (k_ref, v_ref) in enumerate(((kl, vl), (kc, vc), (kr, vr))):
            k = k_ref[low * block : high * block, :]
            s = lax.dot_general(q, k, contract, preferred_element_type=jnp.float32)
            scores.append(s + bias_ref[side, :, first : first + width])
            values.append(v_ref[low * block : high * block, :])
        scores.append(lax.dot_general(q, tk[...], contract, preferred_element_type=jnp.float32))
        values.append(tv[...])
        highest = functools.reduce(
            jnp.maximum, [jnp.max(s, axis=1, keepdims=True) for s in scores]
        )
        total = 0.0
        out = 0.0
        for s, v in zip(scores, values):
            p = jnp.exp2((s - highest) * factor)
            total = total + jnp.sum(p, axis=1, keepdims=True)
            out = out + jnp.dot(p.astype(jnp.bfloat16), v, preferred_element_type=jnp.float32)
        o_ref[n * block : (n + 1) * block, :] = (out / total).astype(o_ref.dtype)


def attend(q, own, left, right, text, head_dim, cols, part, parts):
    rows, inner = q.shape
    block = QROWS * cols
    row_blocks = rows // block
    per = row_blocks // parts
    q_blocks = tuple(range(part * per, (part + 1) * per))
    text_count = text[0].shape[0]
    whole = pl.BlockSpec((rows, head_dim), lambda h: (0, h))
    texts = pl.BlockSpec((text_count, head_dim), lambda h: (0, h))
    pairs = per * block * (9 * block + text_count)
    return pl.pallas_call(
        functools.partial(attn_kernel, q_blocks, row_blocks, cols),
        out_shape=jax.ShapeDtypeStruct((per * block, inner), jnp.bfloat16),
        grid=(inner // head_dim,),
        in_specs=[pl.BlockSpec((per * block, head_dim), lambda h: (part, h))]
        + [whole] * 6
        + [texts] * 2,
        out_specs=pl.BlockSpec((per * block, head_dim), lambda h: (0, h)),
        scratch_shapes=[pltpu.VMEM((3, block, 3 * block), jnp.float32)],
        compiler_params=pltpu.CompilerParams(vmem_limit_bytes=VMEM_LIMIT),
        cost_estimate=pl.CostEstimate(
            flops=4 * pairs * inner,
            bytes_accessed=2 * (6 * rows * inner + 2 * text_count * inner + 2 * per * block * inner),
            transcendentals=pairs * (inner // head_dim),
        ),
    )(q, *own, *left, *right, *text)


def out_kernel(groups, me_ref, *refs):
    a_refs = refs[:groups]
    w_ref, image_ref, gate_ref, bias_ref = refs[groups : groups + 4]
    o_ref = refs[-1]
    inner = a_refs[0].shape[1]
    total = bias_ref[...]
    for k in range(groups):
        row = pl.multiple_of(peer(me_ref[0], k, groups) * inner, inner)
        total = total + jnp.dot(
            a_refs[k][...], w_ref[pl.ds(row, inner), :], preferred_element_type=jnp.float32
        )
    o_ref[...] = (image_ref[...].astype(jnp.float32) + gate_ref[...] * total).astype(o_ref.dtype)


def peer(me, k, groups):
    if groups & (groups - 1) == 0:
        return me ^ k
    return (me + k) % groups


def exchange(block):
    groups = lax.axis_size("head")
    return [block] + [
        lax.ppermute(block, "head", [(peer(i, k, groups), i) for i in range(groups)])
        for k in range(1, groups)
    ]


def output(gathered, w, image, first, gate, bias, before):
    groups = len(gathered)
    rows, inner = gathered[0].shape
    cols = w.shape[1]
    step = 256
    off = first // step
    here = pl.BlockSpec((step, cols), lambda i: (off + i, 0))
    row = pl.BlockSpec((1, cols), lambda i: (0, 0))
    operands = [lax.axis_index("head").astype(jnp.int32).reshape(1), *gathered, w, image]
    operands += [gate.reshape(1, cols), bias.reshape(1, cols)]
    specs = [pl.BlockSpec(memory_space=pltpu.SMEM)]
    specs += [pl.BlockSpec((step, inner), lambda i: (i, 0))] * groups
    specs += [pl.BlockSpec(w.shape, lambda i: (0, 0), pipeline_mode=pl.Buffered(1)), here, row, row]
    aliases = {}
    if before is not None:
        aliases = {len(operands): 0}
        operands.append(before)
        specs.append(pl.BlockSpec(memory_space=pl.ANY))
    return pl.pallas_call(
        functools.partial(out_kernel, groups),
        out_shape=jax.ShapeDtypeStruct(image.shape, jnp.bfloat16),
        grid=(rows // step,),
        in_specs=specs,
        out_specs=here,
        input_output_aliases=aliases,
        compiler_params=pltpu.CompilerParams(vmem_limit_bytes=VMEM_LIMIT),
        cost_estimate=pl.CostEstimate(
            flops=2 * rows * groups * inner * cols,
            bytes_accessed=2 * (groups * inner * (rows + cols) + 2 * rows * cols),
            transcendentals=0,
        ),
    )(*operands)


def body(
    image_tokens,
    conditioning,
    mod_weight,
    mod_bias,
    qkv_weight,
    qkv_bias,
    q_gain,
    k_gain,
    text_kv,
    proj_weight,
    proj_bias,
):
    lat_rows, col_count, model_width = image_tokens.shape
    token_count = lat_rows * col_count
    head_groups = lax.axis_size("head")
    inner_here = qkv_weight.shape[2]
    flat_weight = qkv_weight.reshape(qkv_weight.shape[0], 3 * inner_here)
    gather_rows = functools.partial(lax.all_gather, axis_name="lon", axis=0, tiled=True)
    k_rows = gather_rows(flat_weight[:, inner_here : 2 * inner_here])
    v_rows = gather_rows(flat_weight[:, 2 * inner_here :])
    slice_rows = mod_weight.shape[0]
    row_offset = (lax.axis_index("lon") * head_groups + lax.axis_index("head")) * slice_rows
    silu_part = jax.nn.silu(
        lax.dynamic_slice_in_dim(conditioning, row_offset, slice_rows, 0).astype(jnp.float32)
    )
    partial_mod = jnp.dot(
        silu_part,
        mod_weight.reshape(slice_rows, 3 * model_width).astype(jnp.float32),
        precision=lax.Precision.HIGHEST,
    )
    modulation = lax.psum(partial_mod, ("lon", "head")).reshape(3, model_width) + mod_bias.astype(
        jnp.float32
    )
    modulation, q_here = lax.optimization_barrier((modulation, flat_weight[:, :inner_here]))
    q_rows = gather_rows(q_here)
    token_values = image_tokens.reshape(token_count, model_width).astype(jnp.float32)
    average = jnp.mean(token_values, axis=1, keepdims=True)
    centred = token_values - average
    variance = jnp.mean(centred * centred, axis=1, keepdims=True)
    modulated = (
        (1.0 + modulation[1]) * (centred * lax.rsqrt(variance + 1e-06)) + modulation[0]
    ).astype(jnp.bfloat16)
    local_inner = qkv_weight.shape[2]
    head_dim = q_gain.shape[0]
    bias = qkv_bias.astype(jnp.float32)
    own_k = project(modulated, k_rows, 0, bias[1], k_gain, True)
    own_k, text_here = lax.optimization_barrier((own_k, text_kv))
    text_panel = lax.all_gather(text_here, "lon", axis=1, tiled=True)
    own_v = project(modulated, v_rows, 0, bias[2], k_gain, False)
    own_v, proj_here = lax.optimization_barrier((own_v, proj_weight))
    proj_columns = gather_rows(proj_here)
    count = lax.axis_size("lon")
    up = [(i, (i + 1) % count) for i in range(count)]
    down = [((i + 1) % count, i) for i in range(count)]
    left = (lax.ppermute(own_k, "lon", up), lax.ppermute(own_v, "lon", up))
    right = (lax.ppermute(own_k, "lon", down), lax.ppermute(own_v, "lon", down))
    queries = project(modulated, q_rows, 0, bias[0], q_gain, True)
    out_cols = model_width // head_groups
    col_offset = lax.axis_index("head") * out_cols
    own_image = lax.dynamic_slice_in_dim(
        image_tokens.reshape(token_count, model_width), col_offset, out_cols, 1
    )
    own_gate = lax.dynamic_slice_in_dim(modulation[2], col_offset, out_cols, 0)
    own_bias = lax.dynamic_slice_in_dim(proj_bias, col_offset, out_cols, 0).astype(jnp.float32)
    text = (text_panel[0], text_panel[1])
    parts = lat_rows // QROWS
    rows = token_count // parts
    blocks = []
    for part in range(parts):
        attended = attend(
            queries, (own_k, own_v), left, right, text, head_dim, col_count, part, parts
        )
        blocks.append(exchange(attended))
    block_output = None
    for part, gathered in enumerate(blocks):
        block_output = output(
            gathered, proj_columns, own_image, part * rows, own_gate, own_bias, block_output
        )
    return block_output.reshape(lat_rows, col_count, out_cols)


def solution(mesh):
    placed = (
        P(None, "lon", None),
        P(),
        P(("lon", "head"), None, None),
        P(),
        P("lon", None, "head"),
        P(None, "head"),
        P(),
        P(),
        P(None, "lon", "head"),
        P("lon", "head"),
        P(),
    )
    return jax.shard_map(
        body, mesh=mesh, in_specs=placed, out_specs=P(None, "lon", "head"), check_vma=False
    )
```

```python
import functools
import math

import jax
import jax.numpy as jnp
from jax import lax
from jax.experimental import pallas as pl
from jax.experimental.pallas import tpu as pltpu
from jax.sharding import PartitionSpec as P

RADIUS = 15
QROWS = 16
VMEM_LIMIT = 56 * 1024 * 1024


def proj_kernel(normed, head_dim, x_ref, w_ref, b_ref, g_ref, o_ref):
    rows, width = o_ref.shape
    step = min(256, rows)
    weight = w_ref[...].reshape(x_ref.shape[1], width)

    def one(i, carry):
        at = pl.ds(pl.multiple_of(i * step, step), step)
        raw = jnp.dot(x_ref[at, :], weight, preferred_element_type=jnp.float32) + b_ref[...]
        if normed:
            for h in range(width // head_dim):
                cols = slice(h * head_dim, (h + 1) * head_dim)
                entries = raw[:, cols]
                mean_square = jnp.mean(entries * entries, axis=-1, keepdims=True)
                scaled = entries * lax.rsqrt(mean_square + 1e-06) * g_ref[...]
                o_ref[at, cols] = scaled.astype(o_ref.dtype)
        else:
            o_ref[at, :] = raw.astype(o_ref.dtype)
        return carry

    lax.fori_loop(0, rows // step, one, 0)


def project(x, w, first, bias, gain, normed):
    rows, depth = x.shape
    inner, head_dim = bias.shape[0], gain.shape[0]
    width = 2 * head_dim if inner % (2 * head_dim) == 0 else head_dim
    off = first // width
    return pl.pallas_call(
        functools.partial(proj_kernel, normed, head_dim),
        out_shape=jax.ShapeDtypeStruct((rows, inner), jnp.bfloat16),
        grid=(inner // width,),
        in_specs=[
            pl.BlockSpec((rows, depth), lambda j: (0, 0), pipeline_mode=pl.Buffered(1)),
            pl.BlockSpec((w.shape[0], depth // w.shape[0], width), lambda j: (0, 0, off + j)),
            pl.BlockSpec((1, width), lambda j: (0, j)),
            pl.BlockSpec((1, head_dim), lambda j: (0, 0)),
        ],
        out_specs=pl.BlockSpec((rows, width), lambda j: (0, j)),
        compiler_params=pltpu.CompilerParams(vmem_limit_bytes=VMEM_LIMIT),
        cost_estimate=pl.CostEstimate(
            flops=2 * rows * depth * inner,
            bytes_accessed=2 * (rows * depth + depth * inner + rows * inner),
            transcendentals=0,
        ),
    )(x, w, bias.reshape(1, inner), gain.reshape(1, head_dim))


def attn_kernel(
    q_blocks, row_blocks, cols, q_ref, kc, vc, kl, vl, kr, vr, text, bias_ref, o_ref
):
    block = QROWS * cols
    head_dim = q_ref.shape[1]
    factor = math.log2(math.e) / math.sqrt(head_dim)

    shards, text_rows, _ = text.shape
    each = text_rows // 2
    tk = text[:, :each, :].reshape(shards * each, head_dim)
    tv = text[:, each:, :].reshape(shards * each, head_dim)
    contract = (((1,), (1,)), ((), ()))
    for n, qb in enumerate(q_blocks):
        low, high = max(qb - 1, 0), min(qb + 2, row_blocks)
        first = (low - qb + 1) * block
        width = (high - low) * block
        q = q_ref[n * block : (n + 1) * block, :]
        scores = []
        values = []
        for side, (k_ref, v_ref) in enumerate(((kl, vl), (kc, vc), (kr, vr))):
            k = k_ref[low * block : high * block, :]
            s = lax.dot_general(q, k, contract, preferred_element_type=jnp.float32)
            scores.append(s + bias_ref[side, :, first : first + width])
            values.append(v_ref[low * block : high * block, :])
        scores.append(lax.dot_general(q, tk, contract, preferred_element_type=jnp.float32))
        values.append(tv)
        highest = functools.reduce(
            jnp.maximum, [jnp.max(s, axis=1, keepdims=True) for s in scores]
        )
        total = 0.0
        out = 0.0
        for s, v in zip(scores, values):
            p = jnp.exp2((s - highest) * factor)
            total = total + jnp.sum(p, axis=1, keepdims=True)
            out = out + jnp.dot(p.astype(jnp.bfloat16), v, preferred_element_type=jnp.float32)
        o_ref[n * block : (n + 1) * block, :] = (out / total).astype(o_ref.dtype)


def window_bias(cols):
    block = QROWS * cols
    query = lax.broadcasted_iota(jnp.int32, (3, block, 3 * block), 1)
    key = lax.broadcasted_iota(jnp.int32, (3, block, 3 * block), 2)
    side = lax.broadcasted_iota(jnp.int32, (3, block, 3 * block), 0) - 1
    row_gap = key // cols - QROWS - query // cols
    col_gap = key % cols + side * cols - query % cols
    near = (jnp.abs(row_gap) <= RADIUS) & (jnp.abs(col_gap) <= RADIUS)
    return jnp.where(near, 0.0, -1e30).astype(jnp.float32)


def attend(q, own, left, right, panel, text_rows, window, head_dim, cols, part, parts):
    rows, inner = q.shape
    block = QROWS * cols
    row_blocks = rows // block
    per = row_blocks // parts
    q_blocks = tuple(range(part * per, (part + 1) * per))
    text_count = panel.shape[0] * text_rows // 2
    text_at = panel.shape[1] // text_rows - 1
    whole = pl.BlockSpec((rows, head_dim), lambda h: (0, h))
    texts = pl.BlockSpec((panel.shape[0], text_rows, head_dim), lambda h: (0, text_at, h))
    masks = pl.BlockSpec(window.shape, lambda h: (0, 0, 0), pipeline_mode=pl.Buffered(1))
    pairs = per * block * (9 * block + text_count)
    return pl.pallas_call(
        functools.partial(attn_kernel, q_blocks, row_blocks, cols),
        out_shape=jax.ShapeDtypeStruct((per * block, inner), jnp.bfloat16),
        grid=(inner // head_dim,),
        in_specs=[pl.BlockSpec((per * block, head_dim), lambda h: (part, h))]
        + [whole] * 6
        + [texts, masks],
        out_specs=pl.BlockSpec((per * block, head_dim), lambda h: (0, h)),
        compiler_params=pltpu.CompilerParams(vmem_limit_bytes=VMEM_LIMIT),
        cost_estimate=pl.CostEstimate(
            flops=4 * pairs * inner,
            bytes_accessed=2 * (6 * rows * inner + 2 * text_count * inner + 2 * per * block * inner),
            transcendentals=pairs * (inner // head_dim),
        ),
    )(q, *own, *left, *right, panel, window)


def out_kernel(groups, me_ref, *refs):
    a_refs = refs[:groups]
    w_ref, image_ref, gate_ref, bias_ref = refs[groups : groups + 4]
    o_ref = refs[-1]
    inner = a_refs[0].shape[1]
    total = bias_ref[...]
    for k in range(groups):
        row = pl.multiple_of(peer(me_ref[0], k, groups) * inner, inner)
        total = total + jnp.dot(
            a_refs[k][...], w_ref[pl.ds(row, inner), :], preferred_element_type=jnp.float32
        )
    o_ref[...] = (image_ref[...].astype(jnp.float32) + gate_ref[...] * total).astype(o_ref.dtype)


def peer(me, k, groups):
    if groups & (groups - 1) == 0:
        return me ^ k
    return (me + k) % groups


def exchange(block):
    groups = lax.axis_size("head")
    return [block] + [
        lax.ppermute(block, "head", [(peer(i, k, groups), i) for i in range(groups)])
        for k in range(1, groups)
    ]


def output(gathered, w, image, first, gate, bias, before):
    groups = len(gathered)
    rows, inner = gathered[0].shape
    cols = w.shape[1]
    step = 256
    off = first // step
    here = pl.BlockSpec((step, cols), lambda i: (off + i, 0))
    row = pl.BlockSpec((1, cols), lambda i: (0, 0))
    operands = [lax.axis_index("head").astype(jnp.int32).reshape(1), *gathered, w, image]
    operands += [gate.reshape(1, cols), bias.reshape(1, cols)]
    specs = [pl.BlockSpec(memory_space=pltpu.SMEM)]
    specs += [pl.BlockSpec((step, inner), lambda i: (i, 0))] * groups
    specs += [pl.BlockSpec(w.shape, lambda i: (0, 0), pipeline_mode=pl.Buffered(1)), here, row, row]
    aliases = {}
    if before is not None:
        aliases = {len(operands): 0}
        operands.append(before)
        specs.append(pl.BlockSpec(memory_space=pl.ANY))
    return pl.pallas_call(
        functools.partial(out_kernel, groups),
        out_shape=jax.ShapeDtypeStruct(image.shape, jnp.bfloat16),
        grid=(rows // step,),
        in_specs=specs,
        out_specs=here,
        input_output_aliases=aliases,
        compiler_params=pltpu.CompilerParams(vmem_limit_bytes=VMEM_LIMIT),
        cost_estimate=pl.CostEstimate(
            flops=2 * rows * groups * inner * cols,
            bytes_accessed=2 * (groups * inner * (rows + cols) + 2 * rows * cols),
            transcendentals=0,
        ),
    )(*operands)


def body(
    image_tokens,
    conditioning,
    mod_weight,
    mod_bias,
    qkv_weight,
    qkv_bias,
    q_gain,
    k_gain,
    text_kv,
    proj_weight,
    proj_bias,
):
    lat_rows, col_count, model_width = image_tokens.shape
    token_count = lat_rows * col_count
    head_groups = lax.axis_size("head")
    inner_here = qkv_weight.shape[2]
    flat_weight = qkv_weight.reshape(qkv_weight.shape[0], 3 * inner_here)
    gather_rows = functools.partial(lax.all_gather, axis_name="lon", axis=0, tiled=True)
    kv_rows = gather_rows(flat_weight[:, inner_here:])
    text_rows = 2 * text_kv.shape[1]
    query_text = jnp.concatenate(
        [flat_weight[:, :inner_here], text_kv.reshape(text_rows, inner_here)], axis=0
    )
    out_cols = model_width // head_groups
    col_offset = lax.axis_index("head") * out_cols
    own_image = lax.dynamic_slice_in_dim(
        image_tokens.reshape(token_count, model_width), col_offset, out_cols, 1
    )
    slice_rows = mod_weight.shape[0]
    row_offset = (lax.axis_index("lon") * head_groups + lax.axis_index("head")) * slice_rows
    silu_part = jax.nn.silu(
        lax.dynamic_slice_in_dim(conditioning, row_offset, slice_rows, 0).astype(jnp.float32)
    )
    partial_mod = jnp.dot(
        silu_part,
        mod_weight.reshape(slice_rows, 3 * model_width).astype(jnp.float32),
        precision=lax.Precision.HIGHEST,
    )
    modulation = lax.psum(partial_mod, ("lon", "head")).reshape(3, model_width) + mod_bias.astype(
        jnp.float32
    )
    modulation, query_text, own_image = lax.optimization_barrier(
        (modulation, query_text, own_image)
    )
    panel = lax.all_gather(query_text, "lon", axis=0)
    token_values = image_tokens.reshape(token_count, model_width).astype(jnp.float32)
    average = jnp.mean(token_values, axis=1, keepdims=True)
    centred = token_values - average
    variance = jnp.mean(centred * centred, axis=1, keepdims=True)
    modulated = (
        (1.0 + modulation[1]) * (centred * lax.rsqrt(variance + 1e-06)) + modulation[0]
    ).astype(jnp.bfloat16)
    local_inner = qkv_weight.shape[2]
    head_dim = q_gain.shape[0]
    bias = qkv_bias.astype(jnp.float32)
    own_k = project(modulated, kv_rows[None], 0, bias[1], k_gain, True)
    own_v = project(modulated, kv_rows[None], local_inner, bias[2], k_gain, False)
    own_v, proj_here = lax.optimization_barrier((own_v, proj_weight))
    proj_columns = gather_rows(proj_here)
    count = lax.axis_size("lon")
    up = [(i, (i + 1) % count) for i in range(count)]
    down = [((i + 1) % count, i) for i in range(count)]
    left = (lax.ppermute(own_k, "lon", up), lax.ppermute(own_v, "lon", up))
    right = (lax.ppermute(own_k, "lon", down), lax.ppermute(own_v, "lon", down))
    queries = project(modulated, panel, 0, bias[0], q_gain, True)
    own_gate = lax.dynamic_slice_in_dim(modulation[2], col_offset, out_cols, 0)
    own_bias = lax.dynamic_slice_in_dim(proj_bias, col_offset, out_cols, 0).astype(jnp.float32)
    window = window_bias(col_count)
    parts = lat_rows // QROWS
    rows = token_count // parts
    blocks = []
    for part in range(parts):
        attended = attend(
            queries, (own_k, own_v), left, right, panel, text_rows, window, head_dim, col_count, part, parts
        )
        blocks.append(exchange(attended))
    block_output = None
    for part, gathered in enumerate(blocks):
        block_output = output(
            gathered, proj_columns, own_image, part * rows, own_gate, own_bias, block_output
        )
    return block_output.reshape(lat_rows, col_count, out_cols)


def solution(mesh):
    placed = (
        P(None, "lon", None),
        P(),
        P(("lon", "head"), None, None),
        P(),
        P("lon", None, "head"),
        P(None, "head"),
        P(),
        P(),
        P(None, "lon", "head"),
        P("lon", "head"),
        P(),
    )
    return jax.shard_map(
        body, mesh=mesh, in_specs=placed, out_specs=P(None, "lon", "head"), check_vma=False
    )
```

```python
import functools
import math

import jax
import jax.numpy as jnp
from jax import lax
from jax.experimental import pallas as pl
from jax.experimental.pallas import tpu as pltpu
from jax.sharding import PartitionSpec as P

RADIUS = 15
QROWS = 16
VMEM_LIMIT = 56 * 1024 * 1024


def proj_kernel(normed, head_dim, x_ref, w_ref, b_ref, g_ref, o_ref):
    rows, width = o_ref.shape
    step = min(256, rows)
    weight = w_ref[...].reshape(x_ref.shape[1], width)

    def one(i, carry):
        at = pl.ds(pl.multiple_of(i * step, step), step)
        raw = jnp.dot(x_ref[at, :], weight, preferred_element_type=jnp.float32) + b_ref[...]
        if normed:
            for h in range(width // head_dim):
                cols = slice(h * head_dim, (h + 1) * head_dim)
                entries = raw[:, cols]
                mean_square = jnp.mean(entries * entries, axis=-1, keepdims=True)
                scaled = entries * lax.rsqrt(mean_square + 1e-06) * g_ref[...]
                o_ref[at, cols] = scaled.astype(o_ref.dtype)
        else:
            o_ref[at, :] = raw.astype(o_ref.dtype)
        return carry

    lax.fori_loop(0, rows // step, one, 0)


def project(x, w, first, bias, gain, normed):
    rows, depth = x.shape
    inner, head_dim = bias.shape[0], gain.shape[0]
    width = 2 * head_dim if inner % (2 * head_dim) == 0 else head_dim
    off = first // width
    return pl.pallas_call(
        functools.partial(proj_kernel, normed, head_dim),
        out_shape=jax.ShapeDtypeStruct((rows, inner), jnp.bfloat16),
        grid=(inner // width,),
        in_specs=[
            pl.BlockSpec((rows, depth), lambda j: (0, 0), pipeline_mode=pl.Buffered(1)),
            pl.BlockSpec((w.shape[0], depth // w.shape[0], width), lambda j: (0, 0, off + j)),
            pl.BlockSpec((1, width), lambda j: (0, j)),
            pl.BlockSpec((1, head_dim), lambda j: (0, 0)),
        ],
        out_specs=pl.BlockSpec((rows, width), lambda j: (0, j)),
        compiler_params=pltpu.CompilerParams(vmem_limit_bytes=VMEM_LIMIT),
        cost_estimate=pl.CostEstimate(
            flops=2 * rows * depth * inner,
            bytes_accessed=2 * (rows * depth + depth * inner + rows * inner),
            transcendentals=0,
        ),
    )(x, w, bias.reshape(1, inner), gain.reshape(1, head_dim))


def attn_kernel(
    q_blocks, row_blocks, cols, q_ref, kc, vc, kl, vl, kr, vr, text, bias_ref, o_ref
):
    block = QROWS * cols
    head_dim = q_ref.shape[1]
    factor = math.log2(math.e) / math.sqrt(head_dim)

    shards, text_rows, _ = text.shape
    each = text_rows // 2
    tk = text[:, :each, :].reshape(shards * each, head_dim)
    tv = text[:, each:, :].reshape(shards * each, head_dim)
    contract = (((1,), (1,)), ((), ()))
    for n, qb in enumerate(q_blocks):
        low, high = max(qb - 1, 0), min(qb + 2, row_blocks)
        first = (low - qb + 1) * block
        width = (high - low) * block
        q = q_ref[n * block : (n + 1) * block, :]
        scores = []
        values = []
        for side, (k_ref, v_ref) in enumerate(((kl, vl), (kc, vc), (kr, vr))):
            k = k_ref[low * block : high * block, :]
            s = lax.dot_general(q, k, contract, preferred_element_type=jnp.float32)
            scores.append(s + bias_ref[side, :, first : first + width])
            values.append(v_ref[low * block : high * block, :])
        scores.append(lax.dot_general(q, tk, contract, preferred_element_type=jnp.float32))
        values.append(tv)
        highest = functools.reduce(
            jnp.maximum, [jnp.max(s, axis=1, keepdims=True) for s in scores]
        )
        total = 0.0
        out = 0.0
        for s, v in zip(scores, values):
            p = jnp.exp2((s - highest) * factor)
            total = total + jnp.sum(p, axis=1, keepdims=True)
            out = out + jnp.dot(p.astype(jnp.bfloat16), v, preferred_element_type=jnp.float32)
        o_ref[n * block : (n + 1) * block, :] = (out / total).astype(o_ref.dtype)


def window_bias(cols):
    block = QROWS * cols
    query = lax.broadcasted_iota(jnp.int32, (3, block, 3 * block), 1)
    key = lax.broadcasted_iota(jnp.int32, (3, block, 3 * block), 2)
    side = lax.broadcasted_iota(jnp.int32, (3, block, 3 * block), 0) - 1
    row_gap = key // cols - QROWS - query // cols
    col_gap = key % cols + side * cols - query % cols
    near = (jnp.abs(row_gap) <= RADIUS) & (jnp.abs(col_gap) <= RADIUS)
    return jnp.where(near, 0.0, -1e30).astype(jnp.float32)


def attend(q, own, left, right, panel, text_rows, window, head_dim, cols, part, parts):
    rows, inner = q.shape
    block = QROWS * cols
    row_blocks = rows // block
    per = row_blocks // parts
    q_blocks = tuple(range(part * per, (part + 1) * per))
    text_count = panel.shape[0] * text_rows // 2
    text_at = panel.shape[1] // text_rows - 1
    whole = pl.BlockSpec((rows, head_dim), lambda h: (0, h))
    texts = pl.BlockSpec((panel.shape[0], text_rows, head_dim), lambda h: (0, text_at, h))
    masks = pl.BlockSpec(window.shape, lambda h: (0, 0, 0), pipeline_mode=pl.Buffered(1))
    pairs = per * block * (9 * block + text_count)
    return pl.pallas_call(
        functools.partial(attn_kernel, q_blocks, row_blocks, cols),
        out_shape=jax.ShapeDtypeStruct((per * block, inner), jnp.bfloat16),
        grid=(inner // head_dim,),
        in_specs=[pl.BlockSpec((per * block, head_dim), lambda h: (part, h))]
        + [whole] * 6
        + [texts, masks],
        out_specs=pl.BlockSpec((per * block, head_dim), lambda h: (0, h)),
        compiler_params=pltpu.CompilerParams(vmem_limit_bytes=VMEM_LIMIT),
        cost_estimate=pl.CostEstimate(
            flops=4 * pairs * inner,
            bytes_accessed=2 * (6 * rows * inner + 2 * text_count * inner + 2 * per * block * inner),
            transcendentals=pairs * (inner // head_dim),
        ),
    )(q, *own, *left, *right, panel, window)


def out_kernel(groups, me_ref, *refs):
    a_refs = refs[:groups]
    w_ref, image_ref, gate_ref, bias_ref = refs[groups : groups + 4]
    o_ref = refs[-1]
    inner = a_refs[0].shape[1]
    total = bias_ref[...]
    for k in range(groups):
        row = pl.multiple_of(peer(me_ref[0], k, groups) * inner, inner)
        total = total + jnp.dot(
            a_refs[k][...], w_ref[pl.ds(row, inner), :], preferred_element_type=jnp.float32
        )
    o_ref[...] = (image_ref[...].astype(jnp.float32) + gate_ref[...] * total).astype(o_ref.dtype)


def peer(me, k, groups):
    if groups & (groups - 1) == 0:
        return me ^ k
    return (me + k) % groups


def exchange(block):
    groups = lax.axis_size("head")
    return [block] + [
        lax.ppermute(block, "head", [(peer(i, k, groups), i) for i in range(groups)])
        for k in range(1, groups)
    ]


def output(gathered, w, image, first, gate, bias, before):
    groups = len(gathered)
    rows, inner = gathered[0].shape
    cols = w.shape[1]
    step = 256
    off = first // step
    here = pl.BlockSpec((step, cols), lambda i: (off + i, 0))
    row = pl.BlockSpec((1, cols), lambda i: (0, 0))
    operands = [lax.axis_index("head").astype(jnp.int32).reshape(1), *gathered, w, image]
    operands += [gate.reshape(1, cols), bias.reshape(1, cols)]
    specs = [pl.BlockSpec(memory_space=pltpu.SMEM)]
    specs += [pl.BlockSpec((step, inner), lambda i: (i, 0))] * groups
    specs += [pl.BlockSpec(w.shape, lambda i: (0, 0), pipeline_mode=pl.Buffered(1)), here, row, row]
    aliases = {}
    if before is not None:
        aliases = {len(operands): 0}
        operands.append(before)
        specs.append(pl.BlockSpec(memory_space=pl.ANY))
    return pl.pallas_call(
        functools.partial(out_kernel, groups),
        out_shape=jax.ShapeDtypeStruct(image.shape, jnp.bfloat16),
        grid=(rows // step,),
        in_specs=specs,
        out_specs=here,
        input_output_aliases=aliases,
        compiler_params=pltpu.CompilerParams(vmem_limit_bytes=VMEM_LIMIT),
        cost_estimate=pl.CostEstimate(
            flops=2 * rows * groups * inner * cols,
            bytes_accessed=2 * (groups * inner * (rows + cols) + 2 * rows * cols),
            transcendentals=0,
        ),
    )(*operands)


def body(
    image_tokens,
    conditioning,
    mod_weight,
    mod_bias,
    qkv_weight,
    qkv_bias,
    q_gain,
    k_gain,
    text_kv,
    proj_weight,
    proj_bias,
):
    lat_rows, col_count, model_width = image_tokens.shape
    token_count = lat_rows * col_count
    head_groups = lax.axis_size("head")
    inner_here = qkv_weight.shape[2]
    flat_weight = qkv_weight.reshape(qkv_weight.shape[0], 3 * inner_here)
    gather_rows = functools.partial(lax.all_gather, axis_name="lon", axis=0, tiled=True)
    kv_rows = gather_rows(flat_weight[:, inner_here:])
    text_rows = 2 * text_kv.shape[1]
    query_text = jnp.concatenate(
        [flat_weight[:, :inner_here], text_kv.reshape(text_rows, inner_here)], axis=0
    )
    out_cols = model_width // head_groups
    col_offset = lax.axis_index("head") * out_cols
    own_image = lax.dynamic_slice_in_dim(
        image_tokens.reshape(token_count, model_width), col_offset, out_cols, 1
    )
    slice_rows = mod_weight.shape[0]
    row_offset = (lax.axis_index("lon") * head_groups + lax.axis_index("head")) * slice_rows
    silu_part = jax.nn.silu(
        lax.dynamic_slice_in_dim(conditioning, row_offset, slice_rows, 0).astype(jnp.float32)
    )
    partial_mod = jnp.dot(
        silu_part,
        mod_weight.reshape(slice_rows, 3 * model_width).astype(jnp.float32),
        precision=lax.Precision.HIGHEST,
    )
    modulation = lax.psum(partial_mod, ("lon", "head")).reshape(3, model_width) + mod_bias.astype(
        jnp.float32
    )
    modulation, query_text, own_image = lax.optimization_barrier(
        (modulation, query_text, own_image)
    )
    panel = lax.all_gather(query_text, "lon", axis=0)
    token_values = image_tokens.reshape(token_count, model_width).astype(jnp.float32)
    average = jnp.mean(token_values, axis=1, keepdims=True)
    centred = token_values - average
    variance = jnp.mean(centred * centred, axis=1, keepdims=True)
    modulated = (
        (1.0 + modulation[1]) * (centred * lax.rsqrt(variance + 1e-06)) + modulation[0]
    ).astype(jnp.bfloat16)
    local_inner = qkv_weight.shape[2]
    head_dim = q_gain.shape[0]
    bias = qkv_bias.astype(jnp.float32)
    own_k = project(modulated, kv_rows[None], 0, bias[1], k_gain, True)
    own_v = project(modulated, kv_rows[None], local_inner, bias[2], k_gain, False)
    own_v, proj_here = lax.optimization_barrier((own_v, proj_weight))
    proj_columns = gather_rows(proj_here)
    count = lax.axis_size("lon")
    up = [(i, (i + 1) % count) for i in range(count)]
    down = [((i + 1) % count, i) for i in range(count)]
    left = (lax.ppermute(own_k, "lon", up), lax.ppermute(own_v, "lon", up))
    right = (lax.ppermute(own_k, "lon", down), lax.ppermute(own_v, "lon", down))
    queries = project(modulated, panel, 0, bias[0], q_gain, True)
    own_gate = lax.dynamic_slice_in_dim(modulation[2], col_offset, out_cols, 0)
    own_bias = lax.dynamic_slice_in_dim(proj_bias, col_offset, out_cols, 0).astype(jnp.float32)
    window = window_bias(col_count)
    parts = max(1, lat_rows // (2 * QROWS))
    rows = token_count // parts
    blocks = []
    for part in range(parts):
        attended = attend(
            queries, (own_k, own_v), left, right, panel, text_rows, window, head_dim, col_count, part, parts
        )
        blocks.append(exchange(attended))
    block_output = None
    for part, gathered in enumerate(blocks):
        block_output = output(
            gathered, proj_columns, own_image, part * rows, own_gate, own_bias, block_output
        )
    return block_output.reshape(lat_rows, col_count, out_cols)


def solution(mesh):
    placed = (
        P(None, "lon", None),
        P(),
        P(("lon", "head"), None, None),
        P(),
        P("lon", None, "head"),
        P(None, "head"),
        P(),
        P(),
        P(None, "lon", "head"),
        P("lon", "head"),
        P(),
    )
    return jax.shard_map(
        body, mesh=mesh, in_specs=placed, out_specs=P(None, "lon", "head"), check_vma=False
    )
```
